32 devices in a mesh: occ: 8 (over y, x, core), vir: 4 (over z).
Axes of the slice: x: 2, y: 2, z: 4, core: 2. Of those that a mesh axis runs over, the one named last changes fastest.
Arguments:
- factors: bfloat16 [8, 1024, 2048], P('occ', 'vir'), may hold values from -0.047851562 to 0.047851562
- occupied_energy: float32 [8], replicated, may hold values from -1.5 to -0.5
- virtual_energy: float32 [1024], replicated, may hold values from 0.2 to 3
Outputs:
- dens_vv: float32 [1024, 1024], P(('occ', 'vir'))
- dens_oo: float32 [8, 8], replicated
The draws below stay inside these ranges and needn't reach their ends.
All inputs are finite; a program needn't handle non-finite values.
Results may differ from the reference program's by a relative error of at most 0.0065.
Values may be sent and summed in bfloat16 or wider, within the bound.
No kernel may reach another device: no remote copies, remote signals or barrier semaphores. Data moves between devices by JAX's collectives and lax.ppermute only.
A program may use at most 64 MiB of HBM per device.

```python
import jax
import jax.numpy as jnp
from jax import lax

ORB_DEV = 1
NVIR = 1024
NAUX = 2048
NBATCH = 8
N_OCC = 8


def strengthened(entries, stream_key, source, target, shards_of, factor):
    owner, partner = [(jnp.arange(entries.shape[axis_at]) // (entries.shape[axis_at] // shards_of)).reshape([-1 if axis == axis_at else 1 for axis in range(entries.ndim)]) for axis_at in (source, target)]
    chosen = jax.random.permutation(stream_key, shards_of)[partner]
    strong = (owner == chosen) | (owner == (partner + shards_of // 2) % shards_of)
    return jnp.where(strong, factor * entries, entries)


def block_scale(key, shape, shards, least, top_value):
    def one(position, blocks):
        draws = jax.random.uniform(jax.random.fold_in(jax.random.fold_in(key, 6), position), (blocks,), jnp.float32, least / len(shards), top_value / len(shards))
        return jnp.repeat(jnp.exp(draws), shape[position] // blocks).reshape((-1,) + (1,) * (len(shape) - position - 1))

    factor_of = one(*shards[0])
    for cut in shards[1:]:
        factor_of = factor_of * one(*cut)
    return factor_of


def heavy_noise(rng, dims, deviation, reach, pieces, heavy, held_as=jnp.bfloat16):
    result = deviation * jax.random.normal(rng, dims, jnp.float32)
    if pieces:
        result = result * block_scale(rng, dims, pieces, -0.22, 0.18)
    return jnp.clip(strengthened(result, jax.random.fold_in(rng, 3), *heavy), -reach, reach).astype(held_as)


def setup_inputs(seed: int = 0) -> dict:
    key_list = jax.random.split(jax.random.key(seed), 4)
    factors = heavy_noise(key_list[0], (NBATCH, NVIR, NAUX), 0.008, 0.047851562, ((0, 8), (1, 4)), (0, 1, 8, 2.0))
    occupied_energy = jnp.clip(jax.random.uniform(key_list[1], (NBATCH,), jnp.float32, -1.5, -0.5), -1.5, -0.5)
    virtual_energy = jnp.clip(jax.random.uniform(key_list[2], (NVIR,), jnp.float32, 0.2, 3.0), 0.2, 3.0)
    return dict(factors=factors, occupied_energy=occupied_energy, virtual_energy=virtual_energy)


def reference(factors, occupied_energy, virtual_energy):
    partners = N_OCC // 4
    offsets = jnp.arange(partners, dtype=jnp.int32)
    inner = jnp.arange(ORB_DEV, dtype=jnp.int32)
    columns = jnp.arange(NBATCH, dtype=jnp.int32)
    highest = lax.Precision.HIGHEST

    def per_orbital(carry, orbital):
        vv_total, oo_total = carry
        batch = (orbital // ORB_DEV).astype(jnp.int32)
        partner_ids = (((batch + offsets) % N_OCC)[:, None] * ORB_DEV + inner[None, :]).reshape(-1).astype(jnp.int32)
        left = jnp.take(factors, orbital, axis=0).astype(jnp.float32)
        right = jnp.take(factors, partner_ids, axis=0).astype(jnp.float32)
        integrals = jnp.einsum('ap,jbp->jab', left, right, precision=highest).astype(jnp.bfloat16)
        swapped = jnp.swapaxes(integrals, 1, 2)
        own_energy = jnp.take(occupied_energy, orbital)
        partner_energy = jnp.take(occupied_energy, partner_ids)
        denom = (own_energy + partner_energy[:, None, None]) - virtual_energy[None, :, None] - virtual_energy[None, None, :]
        amps = (integrals.astype(jnp.float32) / denom).astype(jnp.bfloat16)
        tilde = ((2.0 * integrals.astype(jnp.float32) - swapped.astype(jnp.float32)) / denom).astype(jnp.bfloat16)
        vv_term = jnp.einsum('jab,jac->bc', amps.astype(jnp.float32), tilde.astype(jnp.float32), precision=highest)
        gram = -jnp.einsum('jab,kab->jk', amps.astype(jnp.float32), tilde.astype(jnp.float32), precision=highest)
        onehot = (partner_ids[:, None] == columns[None, :]).astype(jnp.float32)
        placed = jnp.dot(onehot.T, jnp.dot(gram, onehot, precision=highest), precision=highest)
        return (vv_total + vv_term, oo_total + placed), None

    start = (jnp.zeros((NVIR, NVIR), jnp.float32), jnp.zeros((NBATCH, NBATCH), jnp.float32))
    (dens_vv, dens_oo), _ = lax.scan(per_orbital, start, jnp.arange(NBATCH, dtype=jnp.int32))
    return dens_vv, dens_oo
```

```python
import functools

import jax
import jax.numpy as jnp
from jax import lax
from jax.experimental import pallas as pl
from jax.experimental.pallas import tpu as pltpu
from jax.sharding import PartitionSpec as P


def from_behind(shard, axis, by):
    length = lax.axis_size(axis)
    return lax.ppermute(shard, axis, [(i, (i + by) % length) for i in range(length)])


def any_mesh(factors, occupied_energy, virtual_energy):
    orbitals = factors.shape[0]
    vblock = factors.shape[1]
    nvir_all = virtual_energy.shape[0]
    nbatch_all = occupied_energy.shape[0]
    occ_count = lax.axis_size("occ")
    vir_count = lax.axis_size("vir")
    partners = occ_count // 4
    occ_pos = lax.axis_index("occ")
    vir_pos = lax.axis_index("vir")
    highest = lax.Precision.HIGHEST
    whole = lax.all_gather(factors, "vir", axis=1, tiled=True)

    def tiles(block):
        return jnp.einsum(
            "sjyp,ixp->isjyx", block, whole, preferred_element_type=jnp.float32
        ).astype(jnp.bfloat16)

    stack = jnp.zeros((orbitals, partners, orbitals, vblock, nvir_all), jnp.bfloat16)
    stack = lax.dynamic_update_slice_in_dim(stack, tiles(factors[None]), 0, 1)

    def advance(position, carry):
        current, filled = carry
        current = from_behind(current, "occ", -1)
        filled = lax.dynamic_update_slice_in_dim(filled, tiles(current[None]), position, 1)
        return (current, filled)

    _, stack = lax.fori_loop(1, partners, advance, (factors, stack))
    sending = stack.reshape(orbitals, partners, orbitals, vblock, vir_count, nvir_all // vir_count)
    received = lax.all_to_all(sending, "vir", split_axis=4, concat_axis=4, tiled=True)
    coulomb = received.transpose(0, 1, 2, 5, 4, 3).reshape(
        orbitals, partners, orbitals, vblock, nvir_all
    )
    batch_ids = (occ_pos + jnp.arange(partners, dtype=jnp.int32)) % occ_count
    global_ids = (
        batch_ids[:, None] * orbitals + jnp.arange(orbitals, dtype=jnp.int32)[None, :]
    ).reshape(-1)
    onehot = (global_ids[:, None] == jnp.arange(nbatch_all, dtype=jnp.int32)[None, :]).astype(
        jnp.float32
    )
    partner_energy = jnp.dot(onehot, occupied_energy, precision=highest).reshape(partners, orbitals)
    own_energy = lax.dynamic_slice_in_dim(occupied_energy, occ_pos * orbitals, orbitals)
    local_vir = lax.dynamic_slice_in_dim(virtual_energy, vir_pos * vblock, vblock)
    denom = (
        own_energy[:, None, None, None, None]
        + partner_energy[None, :, :, None, None]
        - local_vir[:, None]
        - virtual_energy
    )
    amps = (coulomb.astype(jnp.float32) / denom).astype(jnp.bfloat16)
    tilde = ((2.0 * coulomb.astype(jnp.float32) - stack.astype(jnp.float32)) / denom).astype(
        jnp.bfloat16
    )
    flat_amps = amps.reshape(-1, nvir_all)
    flat_tilde = tilde.reshape(-1, nvir_all)
    partial_rows = lax.psum_scatter(
        lax.dot_general(
            flat_amps, flat_tilde, (((0,), (0,)), ((), ())), preferred_element_type=jnp.float32
        ).astype(jnp.bfloat16),
        "occ",
        scatter_dimension=0,
        tiled=True,
    ).astype(jnp.float32)
    dens_vv = lax.psum_scatter(partial_rows, "vir", scatter_dimension=0, tiled=True)
    amps_rows = amps.reshape(orbitals, partners * orbitals, -1)
    tilde_rows = tilde.reshape(orbitals, partners * orbitals, -1)
    gram = -lax.dot_general(
        amps_rows, tilde_rows, (((2,), (2,)), ((0,), (0,))), preferred_element_type=jnp.float32
    )
    gram_sum = jnp.sum(gram, axis=0)
    placed = jnp.dot(onehot.T, jnp.dot(gram_sum, onehot, precision=highest), precision=highest)
    dens_oo = lax.psum(placed, ("occ", "vir"))
    return (dens_vv, dens_oo)


OWN, ACROSS, NEAR, FAR = range(4)


def contract_rows(left, right):
    return lax.dot_general(left, right, (((1,), (1,)), ((), ())), preferred_element_type=jnp.float32)


def pair_kernel(vblock, rows, place_ref, energy_ref, column_ref, row_ref, *refs):
    own_hbm, other_hbm = refs[0:4], refs[4:8]
    keep_ref, send_ref, gram_ref = refs[8:11]
    own_ref, other_ref, same_t, pair_t, pair_a, left_same, left_pair, sems = refs[11:]
    copies = []
    for b in range(4):
        copies.append(pltpu.make_async_copy(own_hbm[b], own_ref.at[b], sems.at[0, b]))
        copies.append(pltpu.make_async_copy(other_hbm[b], other_ref.at[b], sems.at[1, b]))
    for copy in copies:
        copy.start()
    for copy in copies:
        copy.wait()
    gram_ref[...] = jnp.zeros_like(gram_ref)
    same_energy = 2.0 * energy_ref[0]
    pair_energy = energy_ref[0] + energy_ref[1]
    nvir = 4 * vblock

    def fold(product):
        return jnp.sum(product.reshape(vblock // 8, 8, vblock), axis=0)

    def column(p, carry):
        at = pl.ds(pl.multiple_of(p * vblock, vblock), vblock)
        own_all = own_ref[...].reshape(nvir, -1)
        other_all = other_ref[...].reshape(nvir, -1)
        own_p = own_ref[p]
        other_p = other_ref[p]
        straight = contract_rows(own_all, other_p).astype(jnp.bfloat16)
        swapped = contract_rows(other_all, own_p).astype(jnp.bfloat16)
        same = contract_rows(own_all, own_p).astype(jnp.bfloat16)
        across = row_ref[:, at]
        for q in range(4):
            band = slice(q * vblock, (q + 1) * vblock)
            virtual = column_ref[band, :]
            k = straight[band].astype(jnp.float32)
            kt = swapped[band].astype(jnp.float32)
            over = 1.0 / (pair_energy - virtual - across)
            amps = (kt * over).astype(jnp.bfloat16)
            pair_t[band, at] = ((2.0 * k - kt) * over).astype(jnp.bfloat16)
            pair_a[band, at] = amps
            same_amps = (
                same[band].astype(jnp.float32) * (1.0 / (same_energy - virtual - across))
            ).astype(jnp.bfloat16)
            same_t[band, at] = same_amps
            if q in (OWN, NEAR):
                turned = ((2.0 * kt - k) * over).astype(jnp.bfloat16).astype(jnp.float32)
                amps = amps.astype(jnp.float32)
                same_amps = same_amps.astype(jnp.float32)
                gram_ref[0] += fold(same_amps * same_amps)
                gram_ref[1] += fold(same_amps * turned)
                gram_ref[2] += fold(amps * same_amps)
                gram_ref[3] += fold(amps * turned)
        return carry

    lax.fori_loop(0, 4, column, 0)

    half, core = place_ref[0], place_ref[1]
    group = vblock // 2
    for side, out_ref in ((0, keep_ref), (1, send_ref)):
        parity = core if side == 0 else 1 - core
        for q in range(4):
            start = pl.multiple_of(q * vblock + parity * group + half * rows, rows)
            to = slice((side * 4 + q) * rows, (side * 4 + q + 1) * rows)
            left_same[to, :] = same_t[pl.ds(start, rows), :]
            left_pair[to, :] = pair_a[pl.ds(start, rows), :]
    total = jnp.dot(left_same[...], same_t[...], preferred_element_type=jnp.float32) + jnp.dot(
        left_pair[...], pair_t[...], preferred_element_type=jnp.float32
    )
    total = total.astype(jnp.bfloat16)
    for side, out_ref in ((0, keep_ref), (1, send_ref)):
        for q in range(4):
            part = total[(side * 4 + q) * rows : (side * 4 + q + 1) * rows]
            for r in range(4):
                to = pl.multiple_of(place_ref[2 + r] * vblock, vblock)
                out_ref[place_ref[2 + q], :, pl.ds(to, vblock)] = part[
                    :, r * vblock : (r + 1) * vblock
                ]


def pair_terms(place, energy, virtual_local, own_blocks, other_blocks, rows):
    vblock, naux = own_blocks[0].shape
    nvir = 4 * vblock
    smem = pl.BlockSpec(memory_space=pltpu.SMEM)
    vmem = pl.BlockSpec(memory_space=pltpu.VMEM)
    hbm = pl.BlockSpec(memory_space=pl.ANY)
    half = jax.ShapeDtypeStruct((4, rows, nvir), jnp.bfloat16)
    matrix = pltpu.VMEM((nvir, nvir), jnp.bfloat16)
    left = pltpu.VMEM((8 * rows, nvir), jnp.bfloat16)
    return pl.pallas_call(
        functools.partial(pair_kernel, vblock, rows),
        out_shape=(half, half, jax.ShapeDtypeStruct((4, 8, vblock), jnp.float32)),
        in_specs=[smem, smem, vmem, vmem] + [hbm] * 8,
        out_specs=(vmem, vmem, vmem),
        scratch_shapes=[
            pltpu.VMEM((4, vblock, naux), jnp.bfloat16),
            pltpu.VMEM((4, vblock, naux), jnp.bfloat16),
            matrix,
            matrix,
            matrix,
            left,
            left,
            pltpu.SemaphoreType.DMA((2, 4)),
        ],
        compiler_params=pltpu.CompilerParams(vmem_limit_bytes=48 * 1024 * 1024),
        name="pair_terms",
    )(place, energy, virtual_local[:, None], virtual_local[None, :], *own_blocks, *other_blocks)


def middle_levels(factors, occupied_energy, virtual_energy):
    vblock = factors.shape[1]
    nbatch_all = occupied_energy.shape[0]
    occ_count = lax.axis_size("occ")
    occ_pos = lax.axis_index("occ")
    vir_pos = lax.axis_index("vir")
    chips = occ_count // 2
    chip, core = occ_pos // 2, occ_pos % 2
    upper = (vir_pos >= 2).astype(jnp.int32)
    is_middle = (vir_pos == 1) | (vir_pos == 2)
    highest = lax.Precision.HIGHEST
    across = [(1, 2), (2, 1)]
    inward = [(0, 1), (3, 2)]
    outward = [(1, 0), (2, 3)]
    to_far_end = [(1, 3), (2, 0)]

    def over_chips(array, by):
        return lax.ppermute(array, "occ", [(i, i ^ by) for i in range(occ_count)])

    own = factors[0]
    near = lax.ppermute(own, "vir", inward)
    other_mid = lax.ppermute(own, "vir", across)
    far = lax.ppermute(near, "vir", across)
    own_blocks = (own, other_mid, near, far)
    other_blocks = tuple(from_behind(block, "occ", -1) for block in own_blocks)

    order = jnp.where(upper == 1, jnp.array([2, 1, 3, 0]), jnp.array([1, 2, 0, 3])).astype(jnp.int32)
    virtual_local = jnp.take(virtual_energy.reshape(4, vblock), order, axis=0).reshape(-1)
    place = jnp.concatenate([jnp.stack([upper, core]).astype(jnp.int32), order])
    partner_ids = (occ_pos + jnp.arange(2, dtype=jnp.int32)) % occ_count
    energy = jnp.take(occupied_energy, partner_ids)
    rows = vblock * 4 // occ_count // 2
    keep, send, gram = pair_terms(place, energy, virtual_local, own_blocks, other_blocks, rows)

    mine = (
        keep.astype(jnp.float32) + over_chips(send, 1).astype(jnp.float32)
    ).astype(jnp.bfloat16)

    def piece(by):
        return lax.dynamic_index_in_dim(mine, chip ^ by, 0, keepdims=False)

    total = piece(0).astype(jnp.float32)
    for by in range(1, chips):
        total = total + over_chips(piece(by), 2 * by).astype(jnp.float32)
    level = rows // 2
    inner = jnp.where(upper == 1, total[:level], total[level:])
    outer = jnp.where(upper == 1, total[level:], total[:level])
    dens_vv = jnp.where(is_middle, inner, lax.ppermute(outer, "vir", outward))

    onehot = (partner_ids[:, None] == jnp.arange(nbatch_all, dtype=jnp.int32)[None, :]).astype(
        jnp.float32
    )
    gram_sum = jnp.where(is_middle, -jnp.sum(gram, axis=(1, 2)), 0.0).reshape(2, 2)
    placed = jnp.dot(onehot.T, jnp.dot(gram_sum, onehot, precision=highest), precision=highest)
    placed = placed + over_chips(placed, 1)
    of_level = placed
    for by in range(1, chips):
        of_level = of_level + over_chips(placed, 2 * by)
    of_level = jnp.where(is_middle, of_level, 0.0)
    dens_oo = of_level
    for pairs in (across, outward, to_far_end):
        dens_oo = dens_oo + lax.ppermute(of_level, "vir", pairs)
    return dens_vv, dens_oo


def solution(mesh):
    occ_count, vir_count = mesh.shape["occ"], mesh.shape["vir"]
    fits = occ_count // 4 == 2 and vir_count == 4
    return jax.shard_map(
        middle_levels if fits else any_mesh,
        mesh=mesh,
        in_specs=(P("occ", "vir", None), P(), P()),
        out_specs=(P(("occ", "vir"), None), P()),
        check_vma=False,
    )
```
